32 devices in a mesh: cable: 2 (over y), chan: 4 (over z), seg: 2 (over x), freq: 2 (over core).
Axes of the slice: x: 2, y: 2, z: 4, core: 2. Of those that a mesh axis runs over, the one named last changes fastest.
Arguments:
- samples: bfloat16 [512, 16, 8192], P(('cable', 'chan'), 'seg'), parts along dimension 0, may hold values from -24 to 24
- live: int32 [512, 16], P('cable'), parts along dimension 0, may hold values from 0 to 1, as said below
Outputs:
- stack: bfloat16 [512, 64, 2, 256], P(('cable', 'chan', 'seg'), None, None, 'freq'), parts along dimension 0
The draws below stay inside these ranges and needn't reach their ends.
There are 2 independent parts, one for each index of `cable`. The reference program is written for one: setup_inputs(seed, part) draws one part's arguments, and reference() takes and returns one part's arrays. A program takes and returns all parts, laid end to end along the dimension named above; each array names one. Nothing has to cross between parts.
Inputs may be any that keep to these rules, and one draw needn't show every extreme that they name: `live`: 1 marks a usable segment of a channel and 0 an unusable one; in every draw some channels are 0 in every segment.
All inputs are finite; a program needn't handle non-finite values.
Results may differ from the reference program's by a relative error of at most 0.006.
Values may be sent and summed in bfloat16 or wider, within the bound.
No kernel may reach another device: no remote copies, remote signals or barrier semaphores. Data moves between devices by JAX's collectives and lax.ppermute only.
A program may use at most 64 MiB of HBM per device.

```python
import math
import jax
import jax.numpy as jnp
from jax import lax

CH_DEV = 64
SAMPLES = 8192
BINS = 256
OFFSETS = 64
CHANNELS = 256
SEGMENTS = 16
N_CHAN = 4


def draw_samples(key, part):
    base_key = jax.random.fold_in(key, 101)
    scale_key, noise_key = jax.random.split(base_key, 2)
    spread = jnp.exp(jax.random.uniform(scale_key, (CHANNELS, SEGMENTS), jnp.float32, math.log(0.3), math.log(3.0)))
    noise = jax.random.normal(noise_key, (CHANNELS, SEGMENTS, SAMPLES), jnp.float32)
    values = noise * spread[:, :, None]
    return jnp.clip(values, -24.0, 24.0).astype(jnp.bfloat16)


def draw_live(key, part):
    base_key = jax.random.fold_in(key, 202)
    channel_key, segment_key, forced_key = jax.random.split(base_key, 3)
    dead_channel = jax.random.randint(channel_key, (CHANNELS, 1), 0, 16, dtype=jnp.int32) == 0
    dead_segment = jax.random.randint(segment_key, (CHANNELS, SEGMENTS), 0, 8, dtype=jnp.int32) == 0
    forced = jax.random.randint(forced_key, (), 0, CHANNELS, dtype=jnp.int32)
    forced_dead = jnp.arange(CHANNELS, dtype=jnp.int32)[:, None] == forced
    dead = dead_channel | dead_segment | forced_dead
    return jnp.where(dead, 0, 1).astype(jnp.int32)


def setup_inputs(seed: int = 0, part: int = 0) -> dict:
    arg_keys = jax.random.split(jax.random.key(seed), 3)
    own_keys = jax.random.split(jax.random.fold_in(arg_keys[2], part), 3)
    return {
        "samples": draw_samples(jax.random.fold_in(jax.random.fold_in(arg_keys[2], part), 71), part),
        "live": draw_live(jax.random.fold_in(jax.random.fold_in(arg_keys[2], part), 71), part),
    }


EPSILON = 1e-06

def dft_columns(first_bin, count, length):
    sample_index = jnp.arange(length, dtype=jnp.int32)
    bin_index = first_bin + jnp.arange(count, dtype=jnp.int32)
    phase = sample_index[:, None] * bin_index[None, :] % length
    angle = phase.astype(jnp.float32) * (2.0 * math.pi / length)
    return jnp.concatenate([jnp.cos(angle), -jnp.sin(angle)], axis=1).astype(jnp.bfloat16)

def banded(square, row_count):
    band_width = square.shape[1]
    trailing = square.shape[2:]
    flattened = square.reshape((row_count * band_width,) + trailing)
    padding = jnp.zeros((row_count,) + trailing, square.dtype)
    flattened = jnp.concatenate([flattened, padding], axis=0)
    return flattened.reshape((row_count, band_width + 1) + trailing)[:, :OFFSETS]

def reference(samples, live):
    dft_table = dft_columns(1, BINS, SAMPLES).astype(jnp.float32)
    lag_span = OFFSETS - 1

    def transform(block):
        flat_rows = block.reshape(CH_DEV * SEGMENTS, SAMPLES).astype(jnp.float32)
        spectra = jnp.dot(flat_rows, dft_table, precision=lax.Precision.HIGHEST).reshape(CH_DEV, SEGMENTS, 2, BINS)
        energy = lax.optimization_barrier(jnp.sum(spectra * spectra, axis=(2, 3)))
        scaling = lax.rsqrt(energy / (2 * BINS) + EPSILON)
        return spectra * scaling[:, :, None, None]
    blocks = samples.reshape(N_CHAN, CH_DEV, SEGMENTS, SAMPLES)
    scaled = lax.map(transform, blocks).reshape(CHANNELS, SEGMENTS, 2, BINS)
    whitened = (scaled * live.astype(jnp.float32)[:, :, None, None]).astype(jnp.bfloat16)
    padded = jnp.concatenate([whitened, jnp.zeros((lag_span, SEGMENTS, 2, BINS), jnp.bfloat16)], axis=0)
    live_padded = jnp.concatenate([live, jnp.zeros((lag_span, SEGMENTS), jnp.int32)], axis=0)
    conjugate = jnp.array([1.0, -1.0], jnp.float32).reshape(2, 1)

    def stack_block(first_row):
        window = lax.dynamic_slice_in_dim(padded, first_row, CH_DEV + lag_span, 0).astype(jnp.float32)
        live_rows = lax.dynamic_slice_in_dim(live_padded, first_row, CH_DEV + lag_span, 0).astype(jnp.float32)
        owned = window[:CH_DEV]
        real_part = jnp.einsum('iscf,jscf->ijf', owned, window, precision=lax.Precision.HIGHEST)
        imag_part = jnp.einsum('iscf,jscf->ijf', owned * conjugate, window[:, :, ::-1], precision=lax.Precision.HIGHEST)
        pairs = jnp.dot(live_rows[:CH_DEV], live_rows.T, precision=lax.Precision.HIGHEST)
        numerator = jnp.stack([banded(real_part, CH_DEV), banded(imag_part, CH_DEV)], axis=2)
        return (numerator / jnp.maximum(banded(pairs, CH_DEV), 1.0)[:, :, None, None]).astype(jnp.bfloat16)
    starts = jnp.arange(N_CHAN, dtype=jnp.int32) * CH_DEV
    return lax.map(stack_block, starts).reshape(CHANNELS, OFFSETS, 2, BINS)
```

```python
import functools
import math

import jax
import jax.numpy as jnp
import numpy as np
from jax import lax
from jax.experimental import pallas as pl
from jax.experimental.pallas import tpu as pltpu
from jax.sharding import PartitionSpec as P

BINS = 256
OFFSETS = 64
EPSILON = 1e-06
QUARTERS = 4
BASE = 16
LANES = 128
VMEM = pl.BlockSpec(memory_space=pltpu.VMEM)
ANY = pl.BlockSpec(memory_space=pl.ANY)


def rotations(length):
    quarter = length // QUARTERS
    doublings = int(math.log2(quarter // BASE))
    times = np.concatenate(
        [np.arange(BASE), BASE * 2 ** np.arange(doublings), quarter * np.arange(QUARTERS)]
    )
    times = np.concatenate([times, np.zeros(-len(times) % 8, np.int64)])
    angle = (times[:, None] * (1 + np.arange(BINS))[None, :] % length) * (2.0 * math.pi / length)
    table = np.stack([np.cos(angle), np.sin(angle)])
    return np.where(np.abs(table) < 1e-12, 0.0, table).astype(np.float32), doublings


def dft_kernel(doublings, samples, live_t, trig, mine_out, other_out, block, rot, cos_t, sin_t, table, spec, scale, live_col, sem):
    rows = spec.shape[1]
    seg_cols, quarter = mine_out.shape[0] // 2, block.shape[2]
    chans = rows // seg_cols
    freq = lax.axis_index("freq")
    seg = lax.axis_index("seg")
    half = BINS // 2
    row0 = pl.multiple_of(freq * rows, rows)
    rot_copy = pltpu.make_async_copy(trig, rot, sem.at[QUARTERS])
    rot_copy.start()
    copies = []
    for q in range(QUARTERS):
        copy = pltpu.make_async_copy(
            samples.at[pl.ds(row0, rows), pl.ds(q * quarter, quarter)], block.at[q], sem.at[q]
        )
        copy.start()
        copies.append(copy)
    live_col[...] = live_t[...].T.astype(jnp.float32)
    rot_copy.wait()
    cos_t[0:BASE] = rot[0, 0:BASE]
    sin_t[0:BASE] = rot[1, 0:BASE]
    done = BASE
    for step in range(doublings):
        ca, sa = rot[0, BASE + step : BASE + step + 1], rot[1, BASE + step : BASE + step + 1]
        c, s = cos_t[0:done], sin_t[0:done]
        cos_t[done : 2 * done] = c * ca - s * sa
        sin_t[done : 2 * done] = s * ca + c * sa
        done *= 2
    for h in range(2):
        table[:, h * BINS : h * BINS + half] = cos_t[:, h * half : (h + 1) * half].astype(jnp.bfloat16)
        table[:, h * BINS + half : (h + 1) * BINS] = (-sin_t[:, h * half : (h + 1) * half]).astype(jnp.bfloat16)
    first = BASE + doublings
    for q in range(QUARTERS):
        if q % 2 == 0:
            copies[q].wait()
            copies[q + 1].wait()
        part = jnp.dot(block[q], table[...], preferred_element_type=jnp.float32)
        for h in range(2):
            re = part[:, h * BINS : h * BINS + half]
            im = part[:, h * BINS + half : (h + 1) * BINS]
            if q == 0:
                spec[2 * h], spec[2 * h + 1] = re, im
                continue
            al = rot[0, first + q : first + q + 1, h * half : (h + 1) * half]
            be = rot[1, first + q : first + q + 1, h * half : (h + 1) * half]
            spec[2 * h] += re * al + im * be
            spec[2 * h + 1] += im * al - re * be
    squares = jnp.zeros((rows, LANES), jnp.float32)
    for tile in range(4):
        squares += spec[tile] * spec[tile]
    energy = jnp.sum(squares, axis=1, keepdims=True)
    scale[...] = jnp.broadcast_to(lax.rsqrt(energy / (2 * BINS) + EPSILON), scale.shape)
    first_chan = pl.multiple_of(lax.axis_index("chan") * (chans * lax.axis_size("freq")) + freq * chans, chans)
    live = live_col[pl.ds(first_chan, chans), :]
    column = lax.broadcasted_iota(jnp.int32, live.shape, 1)
    for s in range(seg_cols):
        usable = jnp.sum(jnp.where(column == seg * seg_cols + s, live, 0.0), axis=1, keepdims=True)
        factor = scale[pl.ds(s, chans, stride=seg_cols), :]
        for r in range(2):
            for out, h in ((mine_out, freq), (other_out, 1 - freq)):
                value = spec[2 * h + r, pl.ds(s, chans, stride=seg_cols), :]
                out[2 * s + r] = (value * factor * usable).astype(jnp.bfloat16)


def whitened_half(samples, live):
    chan_rows, seg_cols, length = samples.shape
    rows = chan_rows * seg_cols // 2
    trig, doublings = rotations(length)
    quarter = length // QUARTERS
    out = jax.ShapeDtypeStruct((2 * seg_cols, chan_rows // 2, BINS // 2), jnp.bfloat16)
    return pl.pallas_call(
        functools.partial(dft_kernel, doublings),
        in_specs=[ANY, VMEM, ANY],
        out_specs=[VMEM, VMEM],
        out_shape=[out, out],
        scratch_shapes=[
            pltpu.VMEM((QUARTERS, rows, quarter), jnp.bfloat16),
            pltpu.VMEM(trig.shape, jnp.float32),
            pltpu.VMEM((quarter, BINS), jnp.float32),
            pltpu.VMEM((quarter, BINS), jnp.float32),
            pltpu.VMEM((quarter, 2 * BINS), jnp.bfloat16),
            pltpu.VMEM((2 * BINS // LANES, rows, LANES), jnp.float32),
            pltpu.VMEM((rows, LANES), jnp.float32),
            pltpu.VMEM((live.shape[0], live.shape[1]), jnp.float32),
            pltpu.SemaphoreType.DMA((QUARTERS + 1,)),
        ],
        compiler_params=pltpu.CompilerParams(vmem_limit_bytes=48 << 20),
        cost_estimate=pl.CostEstimate(flops=4 * rows * length * BINS, bytes_accessed=2 * rows * length, transcendentals=0),
        name="dft_whiten",
    )(samples.reshape(chan_rows * seg_cols, length), live.T, jnp.asarray(trig))


def cross_kernel(load, owned, inv_t, *refs):
    out, rows_re, rows_im, rows_sum, rows_dif, pairs = refs[-6:]
    load(refs[:-6], rows_re, rows_im)
    segs, width = rows_re.shape[0], rows_re.shape[1]
    for s in range(segs):
        re, im = rows_re[s], rows_im[s]
        rows_sum[s] = re + im
        rows_dif[s] = re - im
    blocks = OFFSETS // 8
    lane = lax.broadcasted_iota(jnp.int32, inv_t.shape, 1)

    def channel(i, carry):
        k1 = [None] * blocks
        k2 = [None] * blocks
        k3 = [None] * blocks
        for s in range(segs):
            a_re = rows_re[s, pl.ds(i, 8, stride=0), :]
            a_sum = rows_sum[s, pl.ds(i, 8, stride=0), :]
            a_dif = rows_dif[s, pl.ds(i, 8, stride=0), :]
            for m in range(blocks):
                at = pl.ds(i + 8 * m, 8)
                t1 = a_re * rows_sum[s, at, :]
                t2 = a_dif * rows_im[s, at, :]
                t3 = a_sum * rows_re[s, at, :]
                k1[m] = t1 if s == 0 else k1[m] + t1
                k2[m] = t2 if s == 0 else k2[m] + t2
                k3[m] = t3 if s == 0 else k3[m] + t3
        inverse = jnp.sum(jnp.where(lane == i, inv_t[...], 0.0), axis=1, keepdims=True)
        for m in range(blocks):
            inv = inverse[8 * m : 8 * m + 8]
            pairs[pl.ds(16 * m, 8, stride=2), :] = (k1[m] - k2[m]) * inv
            pairs[pl.ds(16 * m + 1, 8, stride=2), :] = (k1[m] - k3[m]) * inv
        out[i] = pairs[...].astype(jnp.bfloat16)
        return carry

    lax.fori_loop(0, owned, channel, 0)


def cross_stack(load, arrays, inv_t, owned, segs, width):
    scratch = pltpu.VMEM((segs, width, LANES), jnp.float32)
    bins = arrays[0].shape[-1]
    out = pl.pallas_call(
        functools.partial(cross_kernel, load, owned),
        in_specs=[VMEM] * (1 + len(arrays)),
        out_specs=VMEM,
        out_shape=jax.ShapeDtypeStruct((owned, 2 * OFFSETS, bins), jnp.bfloat16),
        scratch_shapes=[scratch] * 4 + [pltpu.VMEM((2 * OFFSETS, LANES), jnp.float32)],
        compiler_params=pltpu.CompilerParams(vmem_limit_bytes=48 << 20),
        cost_estimate=pl.CostEstimate(flops=8 * owned * OFFSETS * segs * bins, bytes_accessed=owned * OFFSETS * bins * 4, transcendentals=0),
        name="cross",
    )(inv_t, *arrays)
    return out.reshape(owned, OFFSETS, 2, bins)


def inverse_pairs(live, first_row, owned):
    width = owned + OFFSETS
    padded = jnp.concatenate([live, jnp.zeros((OFFSETS, live.shape[1]), live.dtype)], axis=0)
    rows = lax.dynamic_slice_in_dim(padded, first_row, width, 0).astype(jnp.bfloat16)
    square = jnp.dot(rows, rows[:owned].T, preferred_element_type=jnp.float32)
    flat = square.T.reshape(owned * width)
    flat = jnp.concatenate([flat, jnp.zeros((owned,), flat.dtype)])
    band = flat.reshape(owned, width + 1)[:, :OFFSETS]
    return 1.0 / jnp.maximum(band, 1.0).T


def split(value, segs, rows_re, rows_im, first_seg, first_row):
    count = value.shape[1]
    for s in range(segs):
        rows_re[first_seg + s, first_row : first_row + count, :] = value[2 * s].astype(jnp.float32)
        rows_im[first_seg + s, first_row : first_row + count, :] = value[2 * s + 1].astype(jnp.float32)


def load_direct(segs, unit, refs, rows_re, rows_im):
    low, high, both, far, near, next_high = refs
    x = lax.axis_index("seg")
    put = lambda value, group, row: split(value, segs, rows_re, rows_im, group * segs, row * unit)
    for s in range(2 * segs):
        rows_re[s, 3 * unit :, :] = jnp.zeros((8, LANES), jnp.float32)
        rows_im[s, 3 * unit :, :] = jnp.zeros((8, LANES), jnp.float32)

    @pl.when(x == 0)
    def _():
        put(low[...], 0, 0)
        put(high[...], 0, 1)
        put(near[...], 0, 2)
        put(both[...], 1, 0)
        put(far[...], 1, 2)

    @pl.when(x == 1)
    def _():
        put(high[...], 0, 0)
        put(near[...], 0, 1)
        put(next_high[...], 0, 2)
        put(far[...], 1, 0)
        put(both[...], 1, 1)


def direct(low, high, live, unit):
    chan, z = lax.axis_size("chan"), lax.axis_index("chan")
    x = lax.axis_index("seg")
    at = lambda block, group: 2 * block + group
    send = lambda value, pairs: lax.ppermute(value, ("chan", "seg"), pairs)
    to_side = [(at(b, 1), at(b, 0)) for b in range(chan)]
    to_corner = [(at(b, 0), at(b - 1, 1)) for b in range(1, chan)]
    from_side = [(at(b, 0), at(b, 1)) for b in range(chan)]
    from_corner = [(at(b, 1), at(b - 1, 0)) for b in range(1, chan)]
    below = [(at(b, g), at(b - 1, g)) for b in range(1, chan) for g in range(2)]
    below_one = [(at(b, 1), at(b - 1, 1)) for b in range(1, chan)]
    both = send(jnp.concatenate([low, high], axis=1), to_side + to_corner)
    far = send(jnp.where(x == 0, high, low), from_side + from_corner)
    near = send(low, below)
    next_high = send(high, below_one)
    segs = low.shape[0] // 2
    inv_t = inverse_pairs(live, (2 * z + x) * unit, unit)
    return cross_stack(
        functools.partial(load_direct, segs, unit),
        [low, high, both, far, near, next_high],
        inv_t, unit, 2 * segs, 3 * unit + 8,
    )


def load_window(segs, width, refs, rows_re, rows_im):
    (window,) = refs
    for g in range(window.shape[0]):
        split(window[g], segs, rows_re, rows_im, g * segs, 0)
    for s in range(rows_re.shape[0]):
        rows_re[s, width:, :] = jnp.zeros((8, LANES), jnp.float32)
        rows_im[s, width:, :] = jnp.zeros((8, LANES), jnp.float32)


def gathered(low, high, live, owned):
    groups, chan = lax.axis_size("seg"), lax.axis_size("chan")
    own = jnp.concatenate([low, high], axis=1)
    above = lax.ppermute(own[:, :OFFSETS], "chan", [(b, b - 1) for b in range(1, chan)])
    extended = jnp.concatenate([own, above], axis=1)
    width = owned + OFFSETS
    windows = jnp.stack([extended[:, t * owned : t * owned + width] for t in range(groups)])
    window = lax.all_to_all(windows, "seg", split_axis=0, concat_axis=0, tiled=True)
    segs = low.shape[0] // 2
    first_row = (lax.axis_index("chan") * groups + lax.axis_index("seg")) * owned
    inv_t = inverse_pairs(live, first_row, owned)
    return cross_stack(
        functools.partial(load_window, segs, width), [window], inv_t, owned, groups * segs, width + 8
    )


def shards(samples, live):
    mine, other = whitened_half(samples, live)
    theirs = lax.ppermute(other, "freq", [(0, 1), (1, 0)])
    freq = lax.axis_index("freq")
    low = jnp.where(freq == 0, mine, theirs)
    high = jnp.where(freq == 0, theirs, mine)
    groups = lax.axis_size("seg")
    owned = samples.shape[0] // groups
    step = direct if groups == 2 and owned == OFFSETS // 2 else gathered
    return step(low, high, live, owned)


def solution(mesh):
    return jax.shard_map(
        shards,
        mesh=mesh,
        in_specs=(P(("cable", "chan"), "seg", None), P("cable", None)),
        out_specs=P(("cable", "chan", "seg"), None, None, "freq"),
        check_vma=False,
    )
```

```python
import functools
import math

import jax
import jax.numpy as jnp
from jax import lax
from jax.experimental import pallas as pl
from jax.experimental.pallas import tpu as pltpu
from jax.sharding import PartitionSpec as P


BINS = 256
OFFSETS = 64
EPSILON = 1e-06
QUARTERS = 4
BASE = 16
STEP = 32
LANES = 128
VMEM = pl.BlockSpec(memory_space=pltpu.VMEM)
HBM = pl.BlockSpec(memory_space=pltpu.HBM)


def dft_kernel(length, doublings, samples, mine_out, other_out, block, rot, cos_t, sin_t, table, spec, scale, sem):
    rows = spec.shape[1]
    seg_cols, quarter = mine_out.shape[0] // 2, block.shape[2]
    chans = rows // seg_cols
    freq = lax.axis_index("freq")
    half = BINS // 2
    row0 = pl.multiple_of(freq * rows, rows)
    copies = []
    for q in range(QUARTERS):
        copy = pltpu.make_async_copy(
            samples.at[pl.ds(row0, rows), pl.ds(q * quarter, quarter)], block.at[q], sem.at[q]
        )
        copy.start()
        copies.append(copy)
    at = lax.broadcasted_iota(jnp.int32, rot.shape[1:], 0)
    bins = 1 + lax.broadcasted_iota(jnp.int32, rot.shape[1:], 1)
    times = at
    for step in range(doublings):
        times = jnp.where(at == BASE + step, BASE * 2**step, times)
    angle = (times * bins % length).astype(jnp.float32) * (2.0 * math.pi / length)
    rot[0] = jnp.cos(angle)
    rot[1] = jnp.sin(angle)
    cos_t[0:BASE] = rot[0, 0:BASE]
    sin_t[0:BASE] = rot[1, 0:BASE]
    done = BASE
    for step in range(doublings):
        ca, sa = rot[0, BASE + step : BASE + step + 1], rot[1, BASE + step : BASE + step + 1]
        c, s = cos_t[0:done], sin_t[0:done]
        cos_t[done : 2 * done] = c * ca - s * sa
        sin_t[done : 2 * done] = s * ca + c * sa
        done *= 2
    for h in range(2):
        table[:, h * BINS : h * BINS + half] = cos_t[:, h * half : (h + 1) * half].astype(jnp.bfloat16)
        table[:, h * BINS + half : (h + 1) * BINS] = (-sin_t[:, h * half : (h + 1) * half]).astype(jnp.bfloat16)
    turn = (1 + lax.broadcasted_iota(jnp.int32, (1, BINS), 1)) % 4
    for q in range(QUARTERS):
        if q % 2 == 0:
            copies[q].wait()
            copies[q + 1].wait()
        part = jnp.dot(block[q], table[...], preferred_element_type=jnp.float32)
        for h in range(2):
            re = part[:, h * BINS : h * BINS + half]
            im = part[:, h * BINS + half : (h + 1) * BINS]
            if q == 0:
                spec[2 * h], spec[2 * h + 1] = re, im
                continue
            power = turn[:, h * half : (h + 1) * half] * q % 4
            al = jnp.where(power == 0, 1.0, jnp.where(power == 2, -1.0, 0.0))
            be = jnp.where(power == 1, 1.0, jnp.where(power == 3, -1.0, 0.0))
            spec[2 * h] += re * al + im * be
            spec[2 * h + 1] += im * al - re * be
    squares = jnp.zeros((rows, LANES), jnp.float32)
    for tile in range(4):
        squares += spec[tile] * spec[tile]
    energy = jnp.sum(squares, axis=1, keepdims=True)
    scale[...] = jnp.broadcast_to(lax.rsqrt(energy / (2 * BINS) + EPSILON), scale.shape)
    for s in range(seg_cols):
        factor = scale[pl.ds(s, chans, stride=seg_cols), :]
        for r in range(2):
            for out, h in ((mine_out, freq), (other_out, 1 - freq)):
                value = spec[2 * h + r, pl.ds(s, chans, stride=seg_cols), :]
                out[2 * s + r] = (value * factor).astype(jnp.bfloat16)


def whitened_half(samples):
    chan_rows, seg_cols, length = samples.shape
    rows = chan_rows * seg_cols // 2
    quarter = length // QUARTERS
    doublings = int(math.log2(quarter // BASE))
    out = jax.ShapeDtypeStruct((2 * seg_cols, chan_rows // 2, BINS // 2), jnp.bfloat16)
    return pl.pallas_call(
        functools.partial(dft_kernel, length, doublings),
        in_specs=[HBM],
        out_specs=[VMEM, VMEM],
        out_shape=[out, out],
        scratch_shapes=[
            pltpu.VMEM((QUARTERS, rows, quarter), jnp.bfloat16),
            pltpu.VMEM((2, -(-(BASE + doublings) // 8) * 8, BINS), jnp.float32),
            pltpu.VMEM((quarter, BINS), jnp.float32),
            pltpu.VMEM((quarter, BINS), jnp.float32),
            pltpu.VMEM((quarter, 2 * BINS), jnp.bfloat16),
            pltpu.VMEM((2 * BINS // LANES, rows, LANES), jnp.float32),
            pltpu.VMEM((rows, LANES), jnp.float32),
            pltpu.SemaphoreType.DMA((QUARTERS,)),
        ],
        compiler_params=pltpu.CompilerParams(vmem_limit_bytes=48 << 20),
        cost_estimate=pl.CostEstimate(flops=4 * rows * length * BINS, bytes_accessed=2 * rows * length, transcendentals=0),
        name="dft_whiten",
    )(samples.reshape(chan_rows * seg_cols, length))


def cross_kernel(load, last, *refs):
    inverse, before = (refs[0], refs[1]) if last else (None, None)
    out, rows_re, rows_im, rows_sum, rows_dif, pairs = refs[-6:]
    segs = rows_re.shape[0]
    step = pl.program_id(0)

    @pl.when(step == 0)
    def _():
        load(refs[2 if last else 0 : -6], rows_re, rows_im)
        for s in range(segs):
            re, im = rows_re[s], rows_im[s]
            rows_sum[s] = re + im
            rows_dif[s] = re - im

    blocks = OFFSETS // 8

    def channel(n, carry):
        i = step * STEP + n
        k1 = [None] * blocks
        k2 = [None] * blocks
        k3 = [None] * blocks
        for s in range(segs):
            a_re = rows_re[s, pl.ds(i, 8, stride=0), :]
            a_sum = rows_sum[s, pl.ds(i, 8, stride=0), :]
            a_dif = rows_dif[s, pl.ds(i, 8, stride=0), :]
            for m in range(blocks):
                at = pl.ds(i + 8 * m, 8)
                t1 = a_re * rows_sum[s, at, :]
                t2 = a_dif * rows_im[s, at, :]
                t3 = a_sum * rows_re[s, at, :]
                k1[m] = t1 if s == 0 else k1[m] + t1
                k2[m] = t2 if s == 0 else k2[m] + t2
                k3[m] = t3 if s == 0 else k3[m] + t3
        for m in range(blocks):
            at = pl.ds(8 * m, 8)
            re, im = k1[m] - k2[m], k1[m] - k3[m]
            if not last:
                out[0, n, at, :] = re
                out[1, n, at, :] = im
                continue
            inv = inverse[n, at, :]
            pairs[pl.ds(16 * m, 8, stride=2), :] = (re + before[0, n, at, :]) * inv
            pairs[pl.ds(16 * m + 1, 8, stride=2), :] = (im + before[1, n, at, :]) * inv
        if last:
            out[n] = pairs[...].astype(jnp.bfloat16)
        return carry

    lax.fori_loop(0, STEP, channel, 0)


def cross_sums(load, arrays, owned, segs, width, finish=()):
    scratch = pltpu.VMEM((segs, width, LANES), jnp.float32)
    bins = arrays[0].shape[-1]
    result = (
        jax.ShapeDtypeStruct((owned, 2 * OFFSETS, bins), jnp.bfloat16)
        if finish
        else jax.ShapeDtypeStruct((2, owned, OFFSETS, bins), jnp.float32)
    )
    whole = lambda a: pl.BlockSpec(a.shape, lambda n: (0,) * a.ndim, pipeline_mode=pl.Buffered(1))
    sums = pl.BlockSpec((2, STEP, OFFSETS, bins), lambda n: (0, n, 0, 0))
    return pl.pallas_call(
        functools.partial(cross_kernel, load, bool(finish)),
        grid=(owned // STEP,),
        in_specs=([pl.BlockSpec((STEP, OFFSETS, bins), lambda n: (n, 0, 0)), sums] if finish else []) + [whole(a) for a in arrays],
        out_specs=pl.BlockSpec((STEP, 2 * OFFSETS, bins), lambda n: (n, 0, 0)) if finish else sums,
        out_shape=result,
        scratch_shapes=[scratch] * 4 + [pltpu.VMEM((2 * OFFSETS, LANES), jnp.float32)],
        compiler_params=pltpu.CompilerParams(vmem_limit_bytes=32 << 20),
        cost_estimate=pl.CostEstimate(flops=8 * owned * OFFSETS * segs * bins, bytes_accessed=owned * OFFSETS * bins * 4, transcendentals=0),
        name="cross_last" if finish else "cross_first",
    )(*finish, *arrays)


def inverse_pairs(live, first_row, owned):
    width = owned + OFFSETS
    padded = jnp.concatenate([live, jnp.zeros((OFFSETS, live.shape[1]), live.dtype)], axis=0)
    rows = lax.dynamic_slice_in_dim(padded, first_row, width, 0).astype(jnp.bfloat16)
    square = jnp.dot(rows, rows[:owned].T, preferred_element_type=jnp.float32)
    flat = square.T.reshape(owned * width)
    flat = jnp.concatenate([flat, jnp.zeros((owned,), flat.dtype)])
    band = flat.reshape(owned, width + 1)[:, :OFFSETS]
    return jnp.broadcast_to((1.0 / jnp.maximum(band, 1.0))[:, :, None], (owned, OFFSETS, LANES))


def split(value, segs, rows_re, rows_im, first_seg, first_row):
    count = value.shape[1]
    for s in range(segs):
        rows_re[first_seg + s, first_row : first_row + count, :] = value[2 * s].astype(jnp.float32)
        rows_im[first_seg + s, first_row : first_row + count, :] = value[2 * s + 1].astype(jnp.float32)


def clear_tail(rows_re, rows_im, width):
    for s in range(rows_re.shape[0]):
        rows_re[s, width:, :] = jnp.zeros((8, LANES), jnp.float32)
        rows_im[s, width:, :] = jnp.zeros((8, LANES), jnp.float32)


def load_own(segs, unit, refs, rows_re, rows_im):
    low, high, near, next_high = refs
    x = lax.axis_index("seg")
    clear_tail(rows_re, rows_im, 3 * unit)
    put = lambda value, row: split(value, segs, rows_re, rows_im, 0, row * unit)

    @pl.when(x == 0)
    def _():
        put(low[...], 0)
        put(high[...], 1)
        put(near[...], 2)

    @pl.when(x == 1)
    def _():
        put(high[...], 0)
        put(near[...], 1)
        put(next_high[...], 2)


def load_sent(segs, unit, refs, rows_re, rows_im):
    corner, side, swap = refs
    x = lax.axis_index("seg")
    clear_tail(rows_re, rows_im, 3 * unit)
    put = lambda value, row: split(value, segs, rows_re, rows_im, 0, row * unit)

    @pl.when(x == 0)
    def _():
        put(side[...], 0)
        put(swap[...], 1)
        put(corner[...], 2)

    @pl.when(x == 1)
    def _():
        put(swap[...], 0)
        put(corner[...], 1)
        put(side[...], 2)


def direct(low, high, live, unit):
    chan, z = lax.axis_size("chan"), lax.axis_index("chan")
    x = lax.axis_index("seg")
    at = lambda block, group: 2 * block + group
    send = lambda value, pairs: lax.ppermute(value, ("chan", "seg"), pairs)
    blocks, lower = range(chan), range(1, chan)
    across = [(at(b, g), at(b, 1 - g)) for b in blocks for g in range(2)]
    diagonal = [(at(b, g), at(b - 1, 1 - g)) for b in lower for g in range(2)]
    mixed = [(at(b, 1), at(b, 0)) for b in blocks] + [(at(b, 0), at(b - 1, 1)) for b in lower]
    below = [(at(b, g), at(b - 1, g)) for b in lower for g in range(2)]
    below_one = [(at(b, 1), at(b - 1, 1)) for b in lower]
    corner = send(low, diagonal)
    swap = send(high, across)
    near = send(low, below)
    next_high = send(high, below_one)
    side = send(jnp.where(x == 0, high, low), mixed)
    segs = low.shape[0] // 2
    inverse = inverse_pairs(live, (2 * z + x) * unit, unit)
    width = 3 * unit + 8
    near, inverse = lax.optimization_barrier((near, inverse))
    first = cross_sums(functools.partial(load_own, segs, unit), [low, high, near, next_high], unit, segs, width)
    out = cross_sums(functools.partial(load_sent, segs, unit), [corner, side, swap], unit, segs, width, (inverse, first))
    return out.reshape(unit, OFFSETS, 2, out.shape[-1])


def load_window(segs, width, group, refs, rows_re, rows_im):
    (window,) = refs
    split(window[group], segs, rows_re, rows_im, 0, 0)
    clear_tail(rows_re, rows_im, width)


def gathered(low, high, live, owned):
    groups, chan = lax.axis_size("seg"), lax.axis_size("chan")
    own = jnp.concatenate([low, high], axis=1)
    above = lax.ppermute(own[:, :OFFSETS], "chan", [(b, b - 1) for b in range(1, chan)])
    extended = jnp.concatenate([own, above], axis=1)
    width = owned + OFFSETS
    windows = jnp.stack([extended[:, t * owned : t * owned + width] for t in range(groups)])
    window = lax.all_to_all(windows, "seg", split_axis=0, concat_axis=0, tiled=True)
    segs = low.shape[0] // 2
    first_row = (lax.axis_index("chan") * groups + lax.axis_index("seg")) * owned
    inverse = inverse_pairs(live, first_row, owned)
    total = None
    for group in range(groups):
        finish = (inverse, total) if group == groups - 1 else ()
        load = functools.partial(load_window, segs, width, group)
        part = cross_sums(load, [window], owned, segs, width + 8, finish)
        total = part if finish or total is None else total + part
    return total.reshape(owned, OFFSETS, 2, total.shape[-1])


def shards(samples, live):
    mine, other = whitened_half(samples)
    theirs = lax.ppermute(other, "freq", [(0, 1), (1, 0)])
    freq = lax.axis_index("freq")
    rows, cols = samples.shape[:2]
    usable = lax.dynamic_slice(
        live, (lax.axis_index("chan") * rows, lax.axis_index("seg") * cols), (rows, cols)
    )
    usable = jnp.repeat(usable.T.astype(jnp.bfloat16), 2, axis=0)[:, :, None]
    low = jnp.where(freq == 0, mine, theirs) * usable[:, : rows // 2]
    high = jnp.where(freq == 0, theirs, mine) * usable[:, rows // 2 :]
    groups = lax.axis_size("seg")
    owned = samples.shape[0] // groups
    step = direct if groups == 2 and owned == OFFSETS // 2 else gathered
    return step(low, high, live, owned)


def solution(mesh):
    return jax.shard_map(
        shards,
        mesh=mesh,
        in_specs=(P(("cable", "chan"), "seg", None), P("cable", None)),
        out_specs=P(("cable", "chan", "seg"), None, None, "freq"),
        check_vma=False,
    )
```
